32 devices in a mesh: sens: 2 (over x), sx: 4 (over z), sy: 4 (over y, core).
Axes of the slice: x: 2, y: 2, z: 4, core: 2. Of those that a mesh axis runs over, the one named last changes fastest.
Arguments:
- records: bfloat16 [4, 128, 128], P(None, 'sens'), may hold values from -6 to 6
- kernel: bfloat16 [128, 64, 32, 128], P('sens', 'sx', 'sy'), may hold values from -0.09375 to 0.09375
- diffusion: float32 [64, 32], P('sx', 'sy'), may hold values from 0.04 to 0.24
Outputs:
- predicted: float32 [4, 128, 128], P(None, ('sens', 'sx', 'sy'))
The draws below stay inside these ranges and needn't reach their ends.
All inputs are finite; a program needn't handle non-finite values.
Results may differ from the reference program's by a relative error of at most 0.0011.
Values may be sent and summed in bfloat16 or wider, within the bound.
A program may use at most 64 MiB of HBM per device.

```python
import math
import jax
import jax.numpy as jnp
from jax import lax

NT = 128
BATCH = 4
SWEEPS = 4
NS = 128
GX = 64
GY = 32


def draw_records(key, part):
    base = jnp.clip(jax.random.normal(key, (BATCH, NS, NT), jnp.float32), -6.0, 6.0)
    return base.astype(jnp.bfloat16)


def shard_levels(key, shape, split, smallest, largest):
    def one(axis_at, blocks):
        draws = jax.random.uniform(jax.random.fold_in(jax.random.fold_in(key, 6), axis_at), (blocks,), jnp.float32, smallest / len(split), largest / len(split))
        return jnp.repeat(jnp.exp(draws), shape[axis_at] // blocks).reshape((-1,) + (1,) * (len(shape) - axis_at - 1))

    gain = one(*split[0])
    for cut in split[1:]:
        gain = gain * one(*cut)
    return gain


def noise(key, extent, deviation, limit, split=(), held_as=jnp.bfloat16):
    drawn = deviation * jax.random.normal(key, extent, jnp.float32)
    if split:
        drawn = drawn * shard_levels(key, extent, split, -0.22, 0.18)
    return jnp.clip(drawn, -limit, limit).astype(held_as)


def setup_inputs(seed: int = 0) -> dict:
    arg_keys = jax.random.split(jax.random.key(seed), 4)
    records = draw_records(jax.random.fold_in(arg_keys[3], 71), 0)
    kernel = noise(arg_keys[1], (NS, GX, GY, NT), (1.6 / ((NS * GX * GY) ** 0.25 * NT ** 0.5)), 0.09375, ((0, 2), (1, 4), (2, 4)))
    diffusion = jnp.clip(jnp.exp(math.log(0.24) - 1.7917595 * jax.random.uniform(arg_keys[2], (GX, GY), jnp.float32) ** shard_levels(arg_keys[2], (GX, GY), ((0, 4), (1, 4)), -0.2, 0.2)), 0.04, 0.24)
    return dict(records=records, kernel=kernel, diffusion=diffusion)


def smooth(prior_field, diffusion):
    weights = diffusion[None, :, :, None]
    for repeat in range(SWEEPS):
        padded = jnp.pad(prior_field, ((0, 0), (1, 1), (1, 1), (0, 0)))
        beside_all = padded[:, 2:, 1:-1] + padded[:, :-2, 1:-1] + padded[:, 1:-1, 2:] + padded[:, 1:-1, :-2]
        prior_field = prior_field + weights * (beside_all - 4.0 * prior_field)
    return prior_field


def reference(records, kernel, diffusion):
    groups = NS // 64
    kernel_blocks = kernel.reshape(groups, 64, GX * GY, NT)
    data_blocks = records.reshape(BATCH, groups, 64, NT).transpose(1, 0, 2, 3)

    def adjoint_step(running, couple):
        kernel_block, data_block = couple
        portion = lax.conv_general_dilated(
            data_block.astype(jnp.float32), kernel_block.astype(jnp.float32), (1,), [(0, NT - 1)],
            dimension_numbers=("NCH", "IOH", "NCH"), precision=lax.Precision.HIGHEST)
        return running + portion, None

    adjoint_field, _ = lax.scan(adjoint_step, jnp.zeros((BATCH, GX * GY, NT), jnp.float32),
                                (kernel_blocks, data_blocks))
    prior_field = smooth(adjoint_field.reshape(BATCH, GX, GY, NT), diffusion)
    smoothed = prior_field.astype(jnp.bfloat16).astype(jnp.float32)
    flipped = smoothed.reshape(BATCH, GX * GY, NT)[:, :, ::-1]

    def forward_block(kernel_block):
        backward = lax.conv_general_dilated(
            flipped, kernel_block.astype(jnp.float32), (1,), [(0, NT - 1)],
            dimension_numbers=("NCH", "OIH", "NCH"), precision=lax.Precision.HIGHEST)
        return backward[:, :, ::-1]

    results = lax.map(forward_block, kernel_blocks)
    return results.transpose(1, 0, 2, 3).reshape(BATCH, NS, NT)
```

```python
import functools

import jax
import jax.numpy as jnp
from jax import lax
from jax.experimental import pallas as pl
from jax.experimental.pallas import tpu as pltpu
from jax.sharding import PartitionSpec as P

SWEEPS = 4
MESH = pl.DeviceIdType.MESH
F32 = jnp.float32
BF16 = jnp.bfloat16
DIRECTIONS = ((-1, 0), (1, 0), (0, -1), (0, 1), (-1, -1), (-1, 1), (1, -1), (1, 1))


def opposite(d):
    dx, dy = DIRECTIONS[d]
    return DIRECTIONS.index((-dx, -dy))


def lane_iota(rows, window):
    return lax.broadcasted_iota(jnp.int32, (rows, window), 1)


def row_iota(rows, window):
    return lax.broadcasted_iota(jnp.int32, (rows, window), 0)


class Halo:
    def __init__(self, sizes, cells_x, cells_y, margin):
        self.nx, self.ny = sizes
        self.cx, self.cy, self.m = cells_x, cells_y, margin
        half = margin // 2
        low = list(range(half))
        high = [cells_x - margin + i for i in low]
        middle = [i for i in range(margin, cells_x - margin)]
        mid = len(middle) // 2
        self.first = low + high + middle[:mid]
        self.second = [i + half for i in low + high] + middle[mid:]
        self.pairs = len(self.first)
        self.half = half
        self.mx, self.my = lax.axis_index("sx"), lax.axis_index("sy")

    def exists(self, d):
        dx, dy = DIRECTIONS[d]
        ok = jnp.bool_(True)
        if dx:
            ok = ok & (self.mx + dx >= 0) & (self.mx + dx < self.nx)
        if dy:
            ok = ok & (self.my + dy >= 0) & (self.my + dy < self.ny)
        return ok

    def pack(self, centre, packed, fields):
        rows = row_iota(self.cy, centre.shape[-1])
        upper = rows < self.cy // 2
        for f in range(fields):
            for i, (a, b) in enumerate(zip(self.first, self.second)):
                one, two = centre[f, a], pltpu.roll(centre[f, b], self.cy // 2, 0)
                packed[0, f, i] = jnp.where(upper, one, two)
                packed[1, f, i] = jnp.where(upper, two, one)

    def copy(self, d, centre, packed, x_got, y_got, send_sem, recv_sem):
        dx, dy = DIRECTIONS[d]
        o = opposite(d)
        if dy == 0:
            start = 0 if dx < 0 else self.cx - self.m
            src = centre.at[:, pl.ds(start, self.m)]
            dst = x_got.at[0 if dx > 0 else 1]
        else:
            side = packed.at[0 if dy < 0 else 1]
            place = y_got.at[1 if dy < 0 else 0]
            if dx == 0:
                src, dst = side, place.at[:, pl.ds(self.half, self.pairs)]
            else:
                src = side.at[:, pl.ds(0 if dx < 0 else self.half, self.half)]
                dst = place.at[:, pl.ds(0 if dx > 0 else self.half + self.pairs, self.half)]
        return pltpu.make_async_remote_copy(
            src_ref=src, dst_ref=dst, send_sem=send_sem.at[d], recv_sem=recv_sem.at[o],
            device_id={"sx": self.mx + dx, "sy": self.my + dy}, device_id_type=MESH)

    def start(self, *refs):
        for d in range(len(DIRECTIONS)):
            @pl.when(self.exists(d))
            def _():
                self.copy(d, *refs).start()

    def wait(self, *refs):
        for d in range(len(DIRECTIONS)):
            @pl.when(self.exists(d))
            def _():
                self.copy(opposite(d), *refs).wait_recv()
                self.copy(d, *refs).wait_send()

    def clear(self, x_got, y_got):
        x_got[...] = jnp.zeros_like(x_got)
        y_got[...] = jnp.zeros_like(y_got)

    def assemble(self, f, centre, x_got, y_got, wide):
        m, cx, cy = self.m, self.cx, self.cy
        wide[f, pl.ds(m, cx), pl.ds(0, cy)] = centre[f]
        wide[f, pl.ds(0, m), pl.ds(0, cy)] = x_got[0, f]
        wide[f, pl.ds(m + cx, m), pl.ds(0, cy)] = x_got[1, f]
        upper = row_iota(cy, centre.shape[-1]) < cy // 2
        half = self.half
        first = [i - m for i in range(half)] + self.first + [cx + i for i in range(half)]
        second = [i - m + half for i in range(half)] + self.second + [cx + half + i for i in range(half)]
        for i, (a, b) in enumerate(zip(first, second)):
            left, right = y_got[0, f, i], y_got[1, f, i]
            wide[f, m + a, pl.ds(cy, cy)] = jnp.where(upper, right, left)
            wide[f, m + b, pl.ds(cy, cy)] = pltpu.roll(jnp.where(upper, left, right), cy // 2, 0)


def kernel(sizes, vectors, sensors, cells_x, cells_y, window,
           records_ref, rates_ref, kernel_hbm, out_ref,
           kbuf, recf, toep, part, got, field, packed, x_got, y_got, wide,
           d_packed, d_x_got, d_y_got, d_wide, smooth_t, pred, pred_got,
           k_sem, s_send, s_recv, h_send, h_recv, d_send, d_recv, g_send, g_recv, p_send, p_recv):
    n_s, n_x, n_y = sizes
    points = cells_x * cells_y
    chunks = min(n_s, vectors)
    per = vectors // chunks
    margin = SWEEPS
    n_q = n_x * n_y
    group = sensors // n_q
    step = 8
    steps = sensors // step
    me_s, me_x, me_y = lax.axis_index("sens"), lax.axis_index("sx"), lax.axis_index("sy")
    mine = lax.rem(me_s, chunks)
    base = me_s - mine
    me_q = me_x * n_y + me_y

    def k_copy(i):
        return pltpu.make_async_copy(
            kernel_hbm.at[pl.ds(i * step, step)], kbuf.at[pl.ds(i * step, step)], k_sem.at[i])

    for i in range(steps):
        k_copy(i).start()

    halo = Halo((n_x, n_y), cells_x, cells_y, margin)
    halo.clear(x_got, y_got)
    halo.clear(d_x_got, d_y_got)

    barrier = pltpu.get_barrier_semaphore()

    def greet_tile(k, _):
        q = lax.rem(me_q + k, n_q)
        pl.semaphore_signal(barrier, inc=1, device_id={"sx": q // n_y, "sy": lax.rem(q, n_y)}, device_id_type=MESH)
        return 0

    lax.fori_loop(1, n_q, greet_tile, 0)
    for k in range(1, n_s):
        pl.semaphore_signal(barrier, inc=1, device_id={"sens": lax.rem(me_s + k, n_s)}, device_id_type=MESH)

    anti = (lane_iota(window, window) + row_iota(window, window) == window - 1).astype(BF16)
    for v in range(vectors):
        recf[v] = jnp.dot(records_ref[v], anti, preferred_element_type=F32)

    halo.pack(rates_ref, d_packed, 1)

    pack_rows = 16
    lanes16, rows16 = lane_iota(pack_rows, window), row_iota(pack_rows, window)

    def adjoint(chunk, slot, first):
        for v in range(per):
            part[slot, v] = jnp.zeros((points, window), F32)

        def body(i, _):
            if first:
                k_copy(i).wait()
            for v in range(per):
                block = recf[chunk * per + v, pl.ds(pl.multiple_of(i * step, step), step)]
                for s in range(step):
                    line = jnp.broadcast_to(block[s:s + 1], (pack_rows, window))
                    seed = pltpu.roll(line, 0, 1, stride=1, stride_axis=0)
                    seed = jnp.where(lanes16 >= rows16, seed, 0.0)
                    for j in range(window // pack_rows):
                        shifted = seed if j == 0 else jnp.where(
                            lanes16 >= j * pack_rows, pltpu.roll(seed, j * pack_rows, 1), 0.0)
                        toep[pl.ds(s * window + j * pack_rows, pack_rows), pl.ds(v * window, window)] = shifted.astype(BF16)
            lhs = jnp.concatenate([kbuf[i * step + s] for s in range(step)], axis=1)
            res = jnp.dot(lhs, toep[...], preferred_element_type=F32)
            for v in range(per):
                part[slot, v] += res[:, v * window:(v + 1) * window]
            return 0

        lax.fori_loop(0, steps, body, 0)

    def s_copy(k, hop):
        return pltpu.make_async_remote_copy(
            src_ref=part.at[k], dst_ref=got.at[hop - 1], send_sem=s_send.at[hop - 1], recv_sem=s_recv.at[hop - 1],
            device_id={"sens": lax.rem(me_s + hop, n_s)}, device_id_type=MESH)

    halo_d = (rates_ref, d_packed, d_x_got, d_y_got, d_send, d_recv)
    halo_f = (field, packed, x_got, y_got, h_send, h_recv)

    for k in range(1, chunks + 1):
        adjoint(lax.rem(me_s + k, chunks), k - 1, k == 1)
        if k == 1:
            pl.semaphore_wait(barrier, n_q - 1 + n_s - 1)
        for hop in range(k, n_s, chunks):
            s_copy(k - 1, hop).start()
        if k == 1:
            halo.start(*halo_d)

    halo.wait(*halo_d)
    halo.assemble(0, rates_ref, d_x_got, d_y_got, d_wide)

    for hop in range(1, n_s):
        s_copy((hop - 1) % chunks, hop).wait_recv()
    for v in range(per):
        total = part[chunks - 1, v]
        for hop in range(1, n_s):
            total = total + got[hop - 1, v]
        field[v] = total.reshape(cells_x, cells_y, window)
    halo.pack(field, packed, per)
    halo.start(*halo_f)
    halo.wait(*halo_f)
    wide_rows = 2 * cells_y
    for v in range(per):
        halo.assemble(v, field, x_got, y_got, wide)
        now = wide[v]
        for repeat in range(SWEEPS):
            interior = now[1:-1]
            beside = now[2:] + now[:-2] + pltpu.roll(interior, wide_rows - 1, 1) + pltpu.roll(interior, 1, 1)
            rate = d_wide[0, pl.ds(repeat + 1, cells_x + 2 * (margin - repeat - 1))]
            now = interior + rate * (beside - 4.0 * interior)
        done = now[:, :cells_y].reshape(points, window).astype(BF16)
        smooth_t[mine, pl.ds(v * window, window)] = lax.dot_general(
            anti, done, (((1,), (1,)), ((), ())), preferred_element_type=F32).astype(BF16)

    def g_copy(k):
        return pltpu.make_async_remote_copy(
            src_ref=smooth_t.at[mine], dst_ref=smooth_t.at[mine], send_sem=g_send.at[k - 1], recv_sem=g_recv.at[k - 1],
            device_id={"sens": base + lax.rem(mine + k, chunks)}, device_id_type=MESH)

    for k in range(1, chunks):
        g_copy(k).start()

    lanes8, rows8 = lane_iota(8, window), row_iota(8, window)

    def forward(chunk, send):
        def body(i, _):
            q = lax.rem(me_q + 1 + i, n_q)
            rhs = jnp.concatenate([kbuf[q * group + s] for s in range(group)], axis=1)
            res = jnp.dot(smooth_t[chunk], rhs, preferred_element_type=F32)
            lines = []
            for v in range(per):
                for s in range(group):
                    tile = res[v * window:(v + 1) * window, s * window:(s + 1) * window]
                    run = tile[window - 8:]
                    for j in range(window // 8 - 2, -1, -1):
                        run = tile[j * 8:j * 8 + 8] + jnp.where(lanes8 >= 8, pltpu.roll(run, 8, 1), 0.0)
                    run = jnp.where(lanes8 >= rows8, pltpu.roll(run, 0, 1, stride=1, stride_axis=0), 0.0)
                    lines.append(jnp.sum(run, axis=0, keepdims=True))
            pred[chunk, q] = jnp.concatenate(lines, axis=0)
            if send:
                @pl.when(i < n_q - 1)
                def _():
                    p_copy(i + 1).start()
            return 0

        lax.fori_loop(0, n_q, body, 0)

    def p_copy(k):
        q = lax.rem(me_q + k, n_q)
        return pltpu.make_async_remote_copy(
            src_ref=pred.at[:, q], dst_ref=pred_got.at[k - 1], send_sem=p_send.at[k - 1], recv_sem=p_recv.at[k - 1],
            device_id={"sx": q // n_y, "sy": lax.rem(q, n_y)}, device_id_type=MESH)

    forward(mine, chunks == 1)
    for k in range(1, chunks):
        g_copy(k).wait_recv()
        forward(lax.rem(mine - k + chunks, chunks), k == chunks - 1)

    def finish(k, total):
        p_copy(k).wait_recv()
        return total + pred_got[k - 1]

    out_ref[...] = lax.fori_loop(1, n_q, finish, pred[:, me_q])

    def drain(k, _):
        p_copy(k).wait_send()
        return 0

    lax.fori_loop(1, n_q, drain, 0)
    for hop in range(1, n_s):
        s_copy((hop - 1) % chunks, hop).wait_send()
    for k in range(1, chunks):
        g_copy(k).wait_send()


def per_device(sizes, records, kernel_block, diffusion):
    vectors, sensors, window = records.shape
    cells_x, cells_y = diffusion.shape
    points = cells_x * cells_y
    n_s, n_x, n_y = sizes
    n_q = n_x * n_y
    chunks = min(n_s, vectors)
    per = vectors // chunks
    group = sensors // n_q
    margin, pairs, step = SWEEPS, cells_x // 2, 8
    kernel_rows = kernel_block.reshape(sensors, points, window)
    rates = jnp.broadcast_to(diffusion[None, :, :, None], (1, cells_x, cells_y, window))

    def halo_space(fields):
        return [
            pltpu.VMEM((2, fields, pairs, cells_y, window), F32),
            pltpu.VMEM((2, fields, margin, cells_y, window), F32),
            pltpu.VMEM((2, fields, pairs + margin, cells_y, window), F32),
            pltpu.VMEM((fields, cells_x + 2 * margin, 2 * cells_y, window), F32),
        ]

    dma = pltpu.SemaphoreType.DMA
    out = pl.pallas_call(
        functools.partial(kernel, sizes, vectors, sensors, cells_x, cells_y, window),
        out_shape=jax.ShapeDtypeStruct((chunks, per * group, window), F32),
        in_specs=[
            pl.BlockSpec(memory_space=pltpu.VMEM),
            pl.BlockSpec(memory_space=pltpu.VMEM),
            pl.BlockSpec(memory_space=pl.ANY),
        ],
        out_specs=pl.BlockSpec(memory_space=pltpu.VMEM),
        scratch_shapes=[
            pltpu.VMEM((sensors, points, window), BF16),
            pltpu.VMEM((vectors, sensors, window), F32),
            pltpu.VMEM((step * window, per * window), BF16),
            pltpu.VMEM((chunks, per, points, window), F32),
            pltpu.VMEM((max(n_s - 1, 1), per, points, window), F32),
            pltpu.VMEM((per, cells_x, cells_y, window), F32),
            *halo_space(per),
            *halo_space(1),
            pltpu.VMEM((chunks, per * window, points), BF16),
            pltpu.VMEM((chunks, n_q, per * group, window), F32),
            pltpu.VMEM((max(n_q - 1, 1), chunks, per * group, window), F32),
            dma((sensors // step,)),
            *[dma((max(n_s - 1, 1),))] * 2,
            *[dma((len(DIRECTIONS),))] * 4,
            *[dma((max(chunks - 1, 1),))] * 2,
            *[dma((max(n_q - 1, 1),))] * 2,
        ],
        compiler_params=pltpu.CompilerParams(collective_id=0, has_side_effects=True),
    )(records, rates, kernel_rows)
    return out.reshape(vectors, group, window)


def solution(mesh):
    sizes = tuple(mesh.shape[a] for a in ("sens", "sx", "sy"))
    return jax.shard_map(
        functools.partial(per_device, sizes),
        mesh=mesh,
        in_specs=(P(None, "sens", None), P("sens", "sx", "sy", None), P("sx", "sy")),
        out_specs=P(None, ("sens", "sx", "sy"), None),
        check_vma=False,
    )
```

```python
import functools

import jax
import jax.numpy as jnp
from jax import lax
from jax.experimental import pallas as pl
from jax.experimental.pallas import tpu as pltpu
from jax.sharding import PartitionSpec as P

SWEEPS = 4
MESH = pl.DeviceIdType.MESH
F32 = jnp.float32
BF16 = jnp.bfloat16
DIRECTIONS = ((-1, 0), (1, 0), (0, -1), (0, 1), (-1, -1), (-1, 1), (1, -1), (1, 1))


def opposite(d):
    dx, dy = DIRECTIONS[d]
    return DIRECTIONS.index((-dx, -dy))


def lane_iota(rows, window):
    return lax.broadcasted_iota(jnp.int32, (rows, window), 1)


def row_iota(rows, window):
    return lax.broadcasted_iota(jnp.int32, (rows, window), 0)


class Halo:
    def __init__(self, sizes, cells_x, cells_y, margin):
        self.nx, self.ny = sizes
        self.cx, self.cy, self.m = cells_x, cells_y, margin
        half = margin // 2
        low = list(range(half))
        high = [cells_x - margin + i for i in low]
        middle = [i for i in range(margin, cells_x - margin)]
        mid = len(middle) // 2
        self.first = low + high + middle[:mid]
        self.second = [i + half for i in low + high] + middle[mid:]
        self.pairs = len(self.first)
        self.half = half
        self.mx, self.my = lax.axis_index("sx"), lax.axis_index("sy")

    def exists(self, d):
        dx, dy = DIRECTIONS[d]
        ok = jnp.bool_(True)
        if dx:
            ok = ok & (self.mx + dx >= 0) & (self.mx + dx < self.nx)
        if dy:
            ok = ok & (self.my + dy >= 0) & (self.my + dy < self.ny)
        return ok

    def pack(self, centre, packed, fields):
        rows = row_iota(self.cy, centre.shape[-1])
        upper = rows < self.cy // 2
        for f in range(fields):
            for i, (a, b) in enumerate(zip(self.first, self.second)):
                one, two = centre[f, a], pltpu.roll(centre[f, b], self.cy // 2, 0)
                packed[0, f, i] = jnp.where(upper, one, two)
                packed[1, f, i] = jnp.where(upper, two, one)

    def copy(self, d, centre, packed, x_got, y_got, send_sem, recv_sem):
        dx, dy = DIRECTIONS[d]
        o = opposite(d)
        if dy == 0:
            start = 0 if dx < 0 else self.cx - self.m
            src = centre.at[:, pl.ds(start, self.m)]
            dst = x_got.at[0 if dx > 0 else 1]
        else:
            side = packed.at[0 if dy < 0 else 1]
            place = y_got.at[1 if dy < 0 else 0]
            if dx == 0:
                src, dst = side, place.at[:, pl.ds(self.half, self.pairs)]
            else:
                src = side.at[:, pl.ds(0 if dx < 0 else self.half, self.half)]
                dst = place.at[:, pl.ds(0 if dx > 0 else self.half + self.pairs, self.half)]
        return pltpu.make_async_remote_copy(
            src_ref=src, dst_ref=dst, send_sem=send_sem.at[d], recv_sem=recv_sem.at[o],
            device_id={"sx": self.mx + dx, "sy": self.my + dy}, device_id_type=MESH)

    def start(self, *refs):
        for d in range(len(DIRECTIONS)):
            @pl.when(self.exists(d))
            def _():
                self.copy(d, *refs).start()

    def wait(self, *refs):
        for d in range(len(DIRECTIONS)):
            @pl.when(self.exists(d))
            def _():
                self.copy(opposite(d), *refs).wait_recv()
                self.copy(d, *refs).wait_send()

    def clear(self, x_got, y_got):
        x_got[...] = jnp.zeros_like(x_got)
        y_got[...] = jnp.zeros_like(y_got)

    def assemble(self, f, centre, x_got, y_got, wide):
        m, cx, cy = self.m, self.cx, self.cy
        wide[f, pl.ds(m, cx), pl.ds(0, cy)] = centre[f]
        wide[f, pl.ds(0, m), pl.ds(0, cy)] = x_got[0, f]
        wide[f, pl.ds(m + cx, m), pl.ds(0, cy)] = x_got[1, f]
        upper = row_iota(cy, centre.shape[-1]) < cy // 2
        half = self.half
        first = [i - m for i in range(half)] + self.first + [cx + i for i in range(half)]
        second = [i - m + half for i in range(half)] + self.second + [cx + half + i for i in range(half)]
        for i, (a, b) in enumerate(zip(first, second)):
            left, right = y_got[0, f, i], y_got[1, f, i]
            wide[f, m + a, pl.ds(cy, cy)] = jnp.where(upper, right, left)
            wide[f, m + b, pl.ds(cy, cy)] = pltpu.roll(jnp.where(upper, left, right), cy // 2, 0)


def kernel(sizes, vectors, sensors, cells_x, cells_y, window,
           records_ref, rates_ref, kernel_hbm, out_ref,
           kbuf, recf, toep, part, got, field, packed, x_got, y_got, wide,
           d_packed, d_x_got, d_y_got, d_wide, smooth_t, pred, pred_got,
           k_sem, s_send, s_recv, h_send, h_recv, d_send, d_recv, g_send, g_recv, p_send, p_recv):
    n_s, n_x, n_y = sizes
    points = cells_x * cells_y
    chunks = min(n_s, vectors)
    per = vectors // chunks
    margin = SWEEPS
    n_q = n_x * n_y
    group = sensors // n_q
    step = 8
    steps = sensors // step
    me_s, me_x, me_y = lax.axis_index("sens"), lax.axis_index("sx"), lax.axis_index("sy")
    mine = lax.rem(me_s, chunks)
    base = me_s - mine
    me_q = me_x * n_y + me_y

    def k_copy(i):
        return pltpu.make_async_copy(
            kernel_hbm.at[pl.ds(i * step, step)], kbuf.at[pl.ds(i * step, step)], k_sem.at[i])

    for i in range(steps):
        k_copy(i).start()

    halo = Halo((n_x, n_y), cells_x, cells_y, margin)
    halo.clear(x_got, y_got)
    halo.clear(d_x_got, d_y_got)

    barrier = pltpu.get_barrier_semaphore()

    def greet_tile(k, _):
        q = lax.rem(me_q + k, n_q)
        pl.semaphore_signal(barrier, inc=1, device_id={"sx": q // n_y, "sy": lax.rem(q, n_y)}, device_id_type=MESH)
        return 0

    lax.fori_loop(1, n_q, greet_tile, 0)
    for k in range(1, n_s):
        pl.semaphore_signal(barrier, inc=1, device_id={"sens": lax.rem(me_s + k, n_s)}, device_id_type=MESH)

    anti = (lane_iota(window, window) + row_iota(window, window) == window - 1).astype(BF16)
    for v in range(vectors):
        recf[v] = jnp.dot(records_ref[v], anti, preferred_element_type=F32)

    halo.pack(rates_ref, d_packed, 1)

    pack_rows = 16
    lanes16, rows16 = lane_iota(pack_rows, window), row_iota(pack_rows, window)

    def adjoint(chunk, slot, first):
        for v in range(per):
            part[slot, v] = jnp.zeros((points, window), F32)

        def body(i, _):
            if first:
                k_copy(i).wait()
            for v in range(per):
                block = recf[chunk * per + v, pl.ds(pl.multiple_of(i * step, step), step)]
                for s in range(step):
                    line = jnp.broadcast_to(block[s:s + 1], (pack_rows, window))
                    seed = pltpu.roll(line, 0, 1, stride=1, stride_axis=0)
                    seed = jnp.where(lanes16 >= rows16, seed, 0.0)
                    for j in range(window // pack_rows):
                        shifted = seed if j == 0 else jnp.where(
                            lanes16 >= j * pack_rows, pltpu.roll(seed, j * pack_rows, 1), 0.0)
                        toep[pl.ds(s * window + j * pack_rows, pack_rows), pl.ds(v * window, window)] = shifted.astype(BF16)
            lhs = jnp.concatenate([kbuf[i * step + s] for s in range(step)], axis=1)
            res = jnp.dot(lhs, toep[...], preferred_element_type=F32)
            for v in range(per):
                part[slot, v] += res[:, v * window:(v + 1) * window]
            return 0

        lax.fori_loop(0, steps, body, 0)

    def s_copy(k, hop):
        return pltpu.make_async_remote_copy(
            src_ref=part.at[k], dst_ref=got.at[hop - 1], send_sem=s_send.at[hop - 1], recv_sem=s_recv.at[hop - 1],
            device_id={"sens": lax.rem(me_s + hop, n_s)}, device_id_type=MESH)

    halo_d = (rates_ref, d_packed, d_x_got, d_y_got, d_send, d_recv)
    halo_f = (field, packed, x_got, y_got, h_send, h_recv)

    for k in range(1, chunks + 1):
        adjoint(lax.rem(me_s + k, chunks), k - 1, k == 1)
        if k == 1:
            pl.semaphore_wait(barrier, n_q - 1 + n_s - 1)
        for hop in range(k, n_s, chunks):
            s_copy(k - 1, hop).start()
        if k == 1:
            halo.start(*halo_d)

    halo.wait(*halo_d)
    halo.assemble(0, rates_ref, d_x_got, d_y_got, d_wide)

    for hop in range(1, n_s):
        s_copy((hop - 1) % chunks, hop).wait_recv()
    for v in range(per):
        total = part[chunks - 1, v]
        for hop in range(1, n_s):
            total = total + got[hop - 1, v]
        field[v] = total.reshape(cells_x, cells_y, window)
    halo.pack(field, packed, per)
    halo.start(*halo_f)
    halo.wait(*halo_f)
    wide_rows = 2 * cells_y
    for v in range(per):
        halo.assemble(v, field, x_got, y_got, wide)
        now = wide[v]
        for repeat in range(SWEEPS):
            interior = now[1:-1]
            beside = now[2:] + now[:-2] + pltpu.roll(interior, wide_rows - 1, 1) + pltpu.roll(interior, 1, 1)
            rate = d_wide[0, pl.ds(repeat + 1, cells_x + 2 * (margin - repeat - 1))]
            now = interior + rate * (beside - 4.0 * interior)
        done = now[:, :cells_y].reshape(points, window).astype(BF16)
        smooth_t[mine, pl.ds(v * window, window)] = lax.dot_general(
            anti, done, (((1,), (1,)), ((), ())), preferred_element_type=F32).astype(BF16)

    def g_copy(k):
        return pltpu.make_async_remote_copy(
            src_ref=smooth_t.at[mine], dst_ref=smooth_t.at[mine], send_sem=g_send.at[k - 1], recv_sem=g_recv.at[k - 1],
            device_id={"sens": base + lax.rem(mine + k, chunks)}, device_id_type=MESH)

    for k in range(1, chunks):
        g_copy(k).start()

    lanes8, rows8 = lane_iota(8, window), row_iota(8, window)

    unroll = max(u for u in range(1, n_q + 1) if n_q % u == 0 and u * group <= 16)

    def forward(chunk, send):
        def body(i, _):
            for u in range(unroll):
                q = lax.rem(me_q + 1 + i * unroll + u, n_q)
                rhs = jnp.concatenate([kbuf[q * group + s] for s in range(group)], axis=1)
                res = jnp.dot(smooth_t[chunk], rhs, preferred_element_type=F32)
                lines = []
                for v in range(per):
                    for s in range(group):
                        tile = res[v * window:(v + 1) * window, s * window:(s + 1) * window]
                        terms = [tile[:8]]
                        for j in range(1, window // 8):
                            cut = jnp.where(lanes8 < window - 8 * j, tile[8 * j:8 * j + 8], 0.0)
                            terms.append(pltpu.roll(cut, 8 * j, 1))
                        while len(terms) > 1:
                            terms = [a + b for a, b in zip(terms[::2], terms[1::2])]
                        run = jnp.where(lanes8 >= rows8, pltpu.roll(terms[0], 0, 1, stride=1, stride_axis=0), 0.0)
                        lines.append(jnp.sum(run, axis=0, keepdims=True))
                pred[chunk, q] = jnp.concatenate(lines, axis=0)
            if send:
                for u in range(unroll):
                    k = i * unroll + u + 1

                    @pl.when(k < n_q)
                    def _():
                        p_copy(k).start()
            return 0

        lax.fori_loop(0, n_q // unroll, body, 0)

    def p_copy(k):
        q = lax.rem(me_q + k, n_q)
        return pltpu.make_async_remote_copy(
            src_ref=pred.at[:, q], dst_ref=pred_got.at[k - 1], send_sem=p_send.at[k - 1], recv_sem=p_recv.at[k - 1],
            device_id={"sx": q // n_y, "sy": lax.rem(q, n_y)}, device_id_type=MESH)

    forward(mine, chunks == 1)
    for k in range(1, chunks):
        g_copy(k).wait_recv()
        forward(lax.rem(mine - k + chunks, chunks), k == chunks - 1)

    def finish(k, total):
        p_copy(k).wait_recv()
        return total + pred_got[k - 1]

    out_ref[...] = lax.fori_loop(1, n_q, finish, pred[:, me_q])

    def drain(k, _):
        p_copy(k).wait_send()
        return 0

    lax.fori_loop(1, n_q, drain, 0)
    for hop in range(1, n_s):
        s_copy((hop - 1) % chunks, hop).wait_send()
    for k in range(1, chunks):
        g_copy(k).wait_send()


def per_device(sizes, records, kernel_block, diffusion):
    vectors, sensors, window = records.shape
    cells_x, cells_y = diffusion.shape
    points = cells_x * cells_y
    n_s, n_x, n_y = sizes
    n_q = n_x * n_y
    chunks = min(n_s, vectors)
    per = vectors // chunks
    group = sensors // n_q
    margin, pairs, step = SWEEPS, cells_x // 2, 8
    kernel_rows = kernel_block.reshape(sensors, points, window)
    rates = jnp.broadcast_to(diffusion[None, :, :, None], (1, cells_x, cells_y, window))

    def halo_space(fields):
        return [
            pltpu.VMEM((2, fields, pairs, cells_y, window), F32),
            pltpu.VMEM((2, fields, margin, cells_y, window), F32),
            pltpu.VMEM((2, fields, pairs + margin, cells_y, window), F32),
            pltpu.VMEM((fields, cells_x + 2 * margin, 2 * cells_y, window), F32),
        ]

    dma = pltpu.SemaphoreType.DMA
    out = pl.pallas_call(
        functools.partial(kernel, sizes, vectors, sensors, cells_x, cells_y, window),
        out_shape=jax.ShapeDtypeStruct((chunks, per * group, window), F32),
        in_specs=[
            pl.BlockSpec(memory_space=pltpu.VMEM),
            pl.BlockSpec(memory_space=pltpu.VMEM),
            pl.BlockSpec(memory_space=pl.ANY),
        ],
        out_specs=pl.BlockSpec(memory_space=pltpu.VMEM),
        scratch_shapes=[
            pltpu.VMEM((sensors, points, window), BF16),
            pltpu.VMEM((vectors, sensors, window), F32),
            pltpu.VMEM((step * window, per * window), BF16),
            pltpu.VMEM((chunks, per, points, window), F32),
            pltpu.VMEM((max(n_s - 1, 1), per, points, window), F32),
            pltpu.VMEM((per, cells_x, cells_y, window), F32),
            *halo_space(per),
            *halo_space(1),
            pltpu.VMEM((chunks, per * window, points), BF16),
            pltpu.VMEM((chunks, n_q, per * group, window), F32),
            pltpu.VMEM((max(n_q - 1, 1), chunks, per * group, window), F32),
            dma((sensors // step,)),
            *[dma((max(n_s - 1, 1),))] * 2,
            *[dma((len(DIRECTIONS),))] * 4,
            *[dma((max(chunks - 1, 1),))] * 2,
            *[dma((max(n_q - 1, 1),))] * 2,
        ],
        compiler_params=pltpu.CompilerParams(collective_id=0, has_side_effects=True),
    )(records, rates, kernel_rows)
    return out.reshape(vectors, group, window)


def solution(mesh):
    sizes = tuple(mesh.shape[a] for a in ("sens", "sx", "sy"))
    return jax.shard_map(
        functools.partial(per_device, sizes),
        mesh=mesh,
        in_specs=(P(None, "sens", None), P("sens", "sx", "sy", None), P("sx", "sy")),
        out_specs=P(None, ("sens", "sx", "sy"), None),
        check_vma=False,
    )
```

```python
import functools

import jax
import jax.numpy as jnp
from jax import lax
from jax.experimental import pallas as pl
from jax.experimental.pallas import tpu as pltpu
from jax.sharding import PartitionSpec as P

SWEEPS = 4
MESH = pl.DeviceIdType.MESH
F32 = jnp.float32
BF16 = jnp.bfloat16
DIRECTIONS = ((-1, 0), (1, 0), (0, -1), (0, 1), (-1, -1), (-1, 1), (1, -1), (1, 1))


def opposite(d):
    dx, dy = DIRECTIONS[d]
    return DIRECTIONS.index((-dx, -dy))


def lane_iota(rows, window):
    return lax.broadcasted_iota(jnp.int32, (rows, window), 1)


def row_iota(rows, window):
    return lax.broadcasted_iota(jnp.int32, (rows, window), 0)


class Halo:
    def __init__(self, sizes, cells_x, cells_y, margin):
        self.nx, self.ny = sizes
        self.cx, self.cy, self.m = cells_x, cells_y, margin
        half = margin // 2
        low = list(range(half))
        high = [cells_x - margin + i for i in low]
        middle = [i for i in range(margin, cells_x - margin)]
        mid = len(middle) // 2
        self.first = low + high + middle[:mid]
        self.second = [i + half for i in low + high] + middle[mid:]
        self.pairs = len(self.first)
        self.half = half
        self.mx, self.my = lax.axis_index("sx"), lax.axis_index("sy")

    def exists(self, d):
        dx, dy = DIRECTIONS[d]
        ok = jnp.bool_(True)
        if dx:
            ok = ok & (self.mx + dx >= 0) & (self.mx + dx < self.nx)
        if dy:
            ok = ok & (self.my + dy >= 0) & (self.my + dy < self.ny)
        return ok

    def pack(self, centre, packed, fields):
        rows = row_iota(self.cy, centre.shape[-1])
        upper = rows < self.cy // 2
        for f in range(fields):
            for i, (a, b) in enumerate(zip(self.first, self.second)):
                one, two = centre[f, a], pltpu.roll(centre[f, b], self.cy // 2, 0)
                packed[0, f, i] = jnp.where(upper, one, two)
                packed[1, f, i] = jnp.where(upper, two, one)

    def copy(self, d, centre, packed, x_got, y_got, send_sem, recv_sem):
        dx, dy = DIRECTIONS[d]
        o = opposite(d)
        if dy == 0:
            start = 0 if dx < 0 else self.cx - self.m
            src = centre.at[:, pl.ds(start, self.m)]
            dst = x_got.at[0 if dx > 0 else 1]
        else:
            side = packed.at[0 if dy < 0 else 1]
            place = y_got.at[1 if dy < 0 else 0]
            if dx == 0:
                src, dst = side, place.at[:, pl.ds(self.half, self.pairs)]
            else:
                src = side.at[:, pl.ds(0 if dx < 0 else self.half, self.half)]
                dst = place.at[:, pl.ds(0 if dx > 0 else self.half + self.pairs, self.half)]
        return pltpu.make_async_remote_copy(
            src_ref=src, dst_ref=dst, send_sem=send_sem.at[d], recv_sem=recv_sem.at[o],
            device_id={"sx": self.mx + dx, "sy": self.my + dy}, device_id_type=MESH)

    def start(self, *refs):
        for d in range(len(DIRECTIONS)):
            @pl.when(self.exists(d))
            def _():
                self.copy(d, *refs).start()

    def wait(self, *refs):
        for d in range(len(DIRECTIONS)):
            @pl.when(self.exists(d))
            def _():
                self.copy(opposite(d), *refs).wait_recv()
                self.copy(d, *refs).wait_send()

    def clear(self, x_got, y_got):
        x_got[...] = jnp.zeros_like(x_got)
        y_got[...] = jnp.zeros_like(y_got)

    def assemble(self, centre, x_got, y_got, wide):
        m, cx, cy = self.m, self.cx, self.cy
        wide[0, pl.ds(m, cx), pl.ds(0, cy)] = centre[0]
        wide[0, pl.ds(0, m), pl.ds(0, cy)] = x_got[0, 0]
        wide[0, pl.ds(m + cx, m), pl.ds(0, cy)] = x_got[1, 0]
        upper = row_iota(cy, centre.shape[-1]) < cy // 2
        half = self.half
        first = [i - m for i in range(half)] + self.first + [cx + i for i in range(half)]
        second = [i - m + half for i in range(half)] + self.second + [cx + half + i for i in range(half)]
        for i, (a, b) in enumerate(zip(first, second)):
            left, right = y_got[0, 0, i], y_got[1, 0, i]
            wide[0, m + a, pl.ds(cy, cy)] = jnp.where(upper, right, left)
            wide[0, m + b, pl.ds(cy, cy)] = pltpu.roll(jnp.where(upper, left, right), cy // 2, 0)


def kernel(sizes, vectors, sensors, cells_x, cells_y, window,
           records_ref, rates_in, kernel_hbm, out_ref,
           rates_ref, kbuf, recf, toep, part, got, field, packed, x_got, y_got, wide,
           d_packed, d_x_got, d_y_got, d_wide, smooth_t, pred, pred_got,
           k_sem, s_send, s_recv, h_send, h_recv, d_send, d_recv, g_send, g_recv, p_send, p_recv):
    n_s, n_x, n_y = sizes
    points = cells_x * cells_y
    chunks = min(n_s, vectors)
    per = vectors // chunks
    margin = SWEEPS
    n_q = n_x * n_y
    group = sensors // n_q
    step = 8
    steps = sensors // step
    me_s, me_x, me_y = lax.axis_index("sens"), lax.axis_index("sx"), lax.axis_index("sy")
    mine = lax.rem(me_s, chunks)
    base = me_s - mine
    me_q = me_x * n_y + me_y

    def k_copy(i):
        return pltpu.make_async_copy(
            kernel_hbm.at[pl.ds(i * step, step)], kbuf.at[pl.ds(i * step, step)], k_sem.at[i])

    for i in range(steps):
        k_copy(i).start()

    halo = Halo((n_x, n_y), cells_x, cells_y, margin)
    halo.clear(x_got, y_got)
    halo.clear(d_x_got, d_y_got)

    barrier = pltpu.get_barrier_semaphore()

    def greet_tile(k, _):
        q = lax.rem(me_q + k, n_q)
        pl.semaphore_signal(barrier, inc=1, device_id={"sx": q // n_y, "sy": lax.rem(q, n_y)}, device_id_type=MESH)
        return 0

    lax.fori_loop(1, n_q, greet_tile, 0)
    for k in range(1, n_s):
        pl.semaphore_signal(barrier, inc=1, device_id={"sens": lax.rem(me_s + k, n_s)}, device_id_type=MESH)

    anti = (lane_iota(window, window) + row_iota(window, window) == window - 1).astype(BF16)
    for v in range(vectors):
        recf[v] = jnp.dot(records_ref[v], anti, preferred_element_type=F32)

    columns = rates_in[...]
    for x in range(cells_x):
        rates_ref[0, x] = jnp.broadcast_to(columns[:, x:x + 1], (cells_y, window))
    halo.pack(rates_ref, d_packed, 1)

    pack_rows = 16
    lanes16, rows16 = lane_iota(pack_rows, window), row_iota(pack_rows, window)

    def adjoint(chunk, slot, first):
        for v in range(per):
            part[slot, v] = jnp.zeros((points, window), F32)

        def body(i, _):
            if first:
                k_copy(i).wait()
            for v in range(per):
                block = recf[chunk * per + v, pl.ds(pl.multiple_of(i * step, step), step)]
                for s in range(step):
                    line = jnp.broadcast_to(block[s:s + 1], (pack_rows, window))
                    seed = pltpu.roll(line, 0, 1, stride=1, stride_axis=0)
                    seed = jnp.where(lanes16 >= rows16, seed, 0.0)
                    for j in range(window // pack_rows):
                        shifted = seed if j == 0 else jnp.where(
                            lanes16 >= j * pack_rows, pltpu.roll(seed, j * pack_rows, 1), 0.0)
                        toep[pl.ds(s * window + j * pack_rows, pack_rows), pl.ds(v * window, window)] = shifted.astype(BF16)
            lhs = jnp.concatenate([kbuf[i * step + s] for s in range(step)], axis=1)
            res = jnp.dot(lhs, toep[...], preferred_element_type=F32)
            for v in range(per):
                part[slot, v] += res[:, v * window:(v + 1) * window]
            return 0

        lax.fori_loop(0, steps, body, 0)

    def s_copy(k, hop, v):
        return pltpu.make_async_remote_copy(
            src_ref=part.at[k, v], dst_ref=got.at[hop - 1, v],
            send_sem=s_send.at[hop - 1, v], recv_sem=s_recv.at[hop - 1, v],
            device_id={"sens": lax.rem(me_s + hop, n_s)}, device_id_type=MESH)

    halo_d = (rates_ref, d_packed, d_x_got, d_y_got, d_send, d_recv)

    def halo_f(v):
        return tuple(ref.at[v] for ref in (field, packed, x_got, y_got, h_send, h_recv))


    for k in range(1, chunks + 1):
        adjoint(lax.rem(me_s + k, chunks), k - 1, k == 1)
        if k == 1:
            pl.semaphore_wait(barrier, n_q - 1 + n_s - 1)
        for v in range(per):
            for hop in range(k, n_s, chunks):
                s_copy(k - 1, hop, v).start()
        if k == 1:
            halo.start(*halo_d)

    for v in range(per):
        for hop in range(1, n_s):
            s_copy((hop - 1) % chunks, hop, v).wait_recv()
        total = part[chunks - 1, v]
        for hop in range(1, n_s):
            total = total + got[hop - 1, v]
        field[v, 0] = total.reshape(cells_x, cells_y, window)
        halo.pack(field.at[v], packed.at[v], 1)
        halo.start(*halo_f(v))

    halo.wait(*halo_d)
    halo.assemble(rates_ref, d_x_got, d_y_got, d_wide)

    def g_copy(k, v):
        place = smooth_t.at[mine, pl.ds(v * window, window)]
        return pltpu.make_async_remote_copy(
            src_ref=place, dst_ref=place, send_sem=g_send.at[k - 1, v], recv_sem=g_recv.at[k - 1, v],
            device_id={"sens": base + lax.rem(mine + k, chunks)}, device_id_type=MESH)

    wide_rows = 2 * cells_y
    for v in range(per):
        halo.wait(*halo_f(v))
        halo.assemble(field.at[v], x_got.at[v], y_got.at[v], wide)
        now = wide[0]
        for repeat in range(SWEEPS):
            interior = now[1:-1]
            beside = now[2:] + now[:-2] + pltpu.roll(interior, wide_rows - 1, 1) + pltpu.roll(interior, 1, 1)
            rate = d_wide[0, pl.ds(repeat + 1, cells_x + 2 * (margin - repeat - 1))]
            now = interior + rate * (beside - 4.0 * interior)
        done = now[:, :cells_y].reshape(points, window).astype(BF16)
        smooth_t[mine, pl.ds(v * window, window)] = lax.dot_general(
            anti, done, (((1,), (1,)), ((), ())), preferred_element_type=F32).astype(BF16)
        for k in range(1, chunks):
            g_copy(k, v).start()

    lanes8, rows8 = lane_iota(8, window), row_iota(8, window)

    unroll = max(u for u in range(1, n_q + 1) if n_q % u == 0 and u * group <= 16)

    def forward(phase):
        chunk = lax.rem(mine - phase + chunks, chunks)

        def body(i, _):
            for u in range(unroll):
                q = lax.rem(me_q + 1 + i * unroll + u, n_q)
                rhs = jnp.concatenate([kbuf[q * group + s] for s in range(group)], axis=1)
                res = jnp.dot(smooth_t[chunk], rhs, preferred_element_type=F32)
                lines = []
                for v in range(per):
                    for s in range(group):
                        tile = res[v * window:(v + 1) * window, s * window:(s + 1) * window]
                        terms = [tile[:8]]
                        for j in range(1, window // 8):
                            cut = jnp.where(lanes8 < window - 8 * j, tile[8 * j:8 * j + 8], 0.0)
                            terms.append(pltpu.roll(cut, 8 * j, 1))
                        while len(terms) > 1:
                            terms = [a + b for a, b in zip(terms[::2], terms[1::2])]
                        run = jnp.where(lanes8 >= rows8, pltpu.roll(terms[0], 0, 1, stride=1, stride_axis=0), 0.0)
                        lines.append(jnp.sum(run, axis=0, keepdims=True))
                pred[chunk, q] = jnp.concatenate(lines, axis=0)
            for u in range(unroll):
                k = i * unroll + u + 1

                @pl.when(k < n_q)
                def _():
                    p_copy(phase, k).start()
            return 0

        lax.fori_loop(0, n_q // unroll, body, 0)

    def p_copy(phase, k):
        q = lax.rem(me_q + k, n_q)
        chunk = lax.rem(mine - phase + chunks, chunks)
        return pltpu.make_async_remote_copy(
            src_ref=pred.at[chunk, q], dst_ref=pred_got.at[k - 1, chunk],
            send_sem=p_send.at[phase, k - 1], recv_sem=p_recv.at[phase, k - 1],
            device_id={"sx": q // n_y, "sy": lax.rem(q, n_y)}, device_id_type=MESH)

    for phase in range(chunks):
        for v in range(per if phase else 0):
            g_copy(phase, v).wait_recv()
        forward(phase)

    def finish(k, total):
        for phase in range(chunks):
            p_copy(phase, k).wait_recv()
        return total + pred_got[k - 1]

    out_ref[...] = lax.fori_loop(1, n_q, finish, pred[:, me_q])

    def drain(k, _):
        for phase in range(chunks):
            p_copy(phase, k).wait_send()
        return 0

    lax.fori_loop(1, n_q, drain, 0)
    for v in range(per):
        for hop in range(1, n_s):
            s_copy((hop - 1) % chunks, hop, v).wait_send()
        for k in range(1, chunks):
            g_copy(k, v).wait_send()


def per_device(sizes, records, kernel_block, diffusion):
    vectors, sensors, window = records.shape
    cells_x, cells_y = diffusion.shape
    points = cells_x * cells_y
    n_s, n_x, n_y = sizes
    n_q = n_x * n_y
    chunks = min(n_s, vectors)
    per = vectors // chunks
    group = sensors // n_q
    margin, pairs, step = SWEEPS, cells_x // 2, 8
    kernel_rows = kernel_block.reshape(sensors, points, window)
    rates = diffusion.T

    def halo_space(lead):
        return [
            pltpu.VMEM((*lead, 2, 1, pairs, cells_y, window), F32),
            pltpu.VMEM((*lead, 2, 1, margin, cells_y, window), F32),
            pltpu.VMEM((*lead, 2, 1, pairs + margin, cells_y, window), F32),
            pltpu.VMEM((1, cells_x + 2 * margin, 2 * cells_y, window), F32),
        ]

    dma = pltpu.SemaphoreType.DMA
    out = pl.pallas_call(
        functools.partial(kernel, sizes, vectors, sensors, cells_x, cells_y, window),
        out_shape=jax.ShapeDtypeStruct((chunks, per * group, window), F32),
        in_specs=[
            pl.BlockSpec(memory_space=pltpu.VMEM),
            pl.BlockSpec(memory_space=pltpu.VMEM),
            pl.BlockSpec(memory_space=pl.ANY),
        ],
        out_specs=pl.BlockSpec(memory_space=pltpu.VMEM),
        scratch_shapes=[
            pltpu.VMEM((1, cells_x, cells_y, window), F32),
            pltpu.VMEM((sensors, points, window), BF16),
            pltpu.VMEM((vectors, sensors, window), F32),
            pltpu.VMEM((step * window, per * window), BF16),
            pltpu.VMEM((chunks, per, points, window), F32),
            pltpu.VMEM((max(n_s - 1, 1), per, points, window), F32),
            pltpu.VMEM((per, 1, cells_x, cells_y, window), F32),
            *halo_space((per,)),
            *halo_space(()),
            pltpu.VMEM((chunks, per * window, points), BF16),
            pltpu.VMEM((chunks, n_q, per * group, window), F32),
            pltpu.VMEM((max(n_q - 1, 1), chunks, per * group, window), F32),
            dma((sensors // step,)),
            *[dma((max(n_s - 1, 1), per))] * 2,
            *[dma((per, len(DIRECTIONS)))] * 2,
            *[dma((len(DIRECTIONS),))] * 2,
            *[dma((max(chunks - 1, 1), per))] * 2,
            *[dma((chunks, max(n_q - 1, 1)))] * 2,
        ],
        compiler_params=pltpu.CompilerParams(collective_id=0, has_side_effects=True),
    )(records, rates, kernel_rows)
    return out.reshape(vectors, group, window)


def solution(mesh):
    sizes = tuple(mesh.shape[a] for a in ("sens", "sx", "sy"))
    return jax.shard_map(
        functools.partial(per_device, sizes),
        mesh=mesh,
        in_specs=(P(None, "sens", None), P("sens", "sx", "sy", None), P("sx", "sy")),
        out_specs=P(None, ("sens", "sx", "sy"), None),
        check_vma=False,
    )
```

```python
import functools

import jax
import jax.numpy as jnp
from jax import lax
from jax.experimental import pallas as pl
from jax.experimental.pallas import tpu as pltpu
from jax.sharding import PartitionSpec as P

SWEEPS = 4
MESH = pl.DeviceIdType.MESH
F32 = jnp.float32
BF16 = jnp.bfloat16
DIRECTIONS = ((-1, 0), (1, 0), (0, -1), (0, 1), (-1, -1), (-1, 1), (1, -1), (1, 1))


def opposite(d):
    dx, dy = DIRECTIONS[d]
    return DIRECTIONS.index((-dx, -dy))


def lane_iota(rows, window):
    return lax.broadcasted_iota(jnp.int32, (rows, window), 1)


def row_iota(rows, window):
    return lax.broadcasted_iota(jnp.int32, (rows, window), 0)


class Halo:
    def __init__(self, sizes, cells_x, cells_y, margin):
        self.nx, self.ny = sizes
        self.cx, self.cy, self.m = cells_x, cells_y, margin
        half = margin // 2
        low = list(range(half))
        high = [cells_x - margin + i for i in low]
        middle = [i for i in range(margin, cells_x - margin)]
        mid = len(middle) // 2
        self.first = low + high + middle[:mid]
        self.second = [i + half for i in low + high] + middle[mid:]
        self.pairs = len(self.first)
        self.half = half
        self.mx, self.my = lax.axis_index("sx"), lax.axis_index("sy")

    def exists(self, d):
        dx, dy = DIRECTIONS[d]
        ok = jnp.bool_(True)
        if dx:
            ok = ok & (self.mx + dx >= 0) & (self.mx + dx < self.nx)
        if dy:
            ok = ok & (self.my + dy >= 0) & (self.my + dy < self.ny)
        return ok

    def pack(self, centre, packed, fields):
        rows = row_iota(self.cy, centre.shape[-1])
        upper = rows < self.cy // 2
        for f in range(fields):
            for i, (a, b) in enumerate(zip(self.first, self.second)):
                one, two = centre[f, a], pltpu.roll(centre[f, b], self.cy // 2, 0)
                packed[0, f, i] = jnp.where(upper, one, two)
                packed[1, f, i] = jnp.where(upper, two, one)

    def copy(self, d, centre, packed, x_got, y_got, send_sem, recv_sem):
        dx, dy = DIRECTIONS[d]
        o = opposite(d)
        if dy == 0:
            start = 0 if dx < 0 else self.cx - self.m
            src = centre.at[:, pl.ds(start, self.m)]
            dst = x_got.at[0 if dx > 0 else 1]
        else:
            side = packed.at[0 if dy < 0 else 1]
            place = y_got.at[1 if dy < 0 else 0]
            if dx == 0:
                src, dst = side, place.at[:, pl.ds(self.half, self.pairs)]
            else:
                src = side.at[:, pl.ds(0 if dx < 0 else self.half, self.half)]
                dst = place.at[:, pl.ds(0 if dx > 0 else self.half + self.pairs, self.half)]
        return pltpu.make_async_remote_copy(
            src_ref=src, dst_ref=dst, send_sem=send_sem.at[d], recv_sem=recv_sem.at[o],
            device_id={"sx": self.mx + dx, "sy": self.my + dy}, device_id_type=MESH)

    def start(self, *refs):
        for d in range(len(DIRECTIONS)):
            @pl.when(self.exists(d))
            def _():
                self.copy(d, *refs).start()

    def wait(self, *refs):
        for d in range(len(DIRECTIONS)):
            @pl.when(self.exists(d))
            def _():
                self.copy(opposite(d), *refs).wait_recv()
                self.copy(d, *refs).wait_send()

    def clear(self, x_got, y_got):
        x_got[...] = jnp.zeros_like(x_got)
        y_got[...] = jnp.zeros_like(y_got)

    def assemble(self, centre, x_got, y_got, wide):
        m, cx, cy = self.m, self.cx, self.cy
        wide[0, pl.ds(m, cx), pl.ds(0, cy)] = centre[0]
        wide[0, pl.ds(0, m), pl.ds(0, cy)] = x_got[0, 0]
        wide[0, pl.ds(m + cx, m), pl.ds(0, cy)] = x_got[1, 0]
        upper = row_iota(cy, centre.shape[-1]) < cy // 2
        half = self.half
        first = [i - m for i in range(half)] + self.first + [cx + i for i in range(half)]
        second = [i - m + half for i in range(half)] + self.second + [cx + half + i for i in range(half)]
        for i, (a, b) in enumerate(zip(first, second)):
            left, right = y_got[0, 0, i], y_got[1, 0, i]
            wide[0, m + a, pl.ds(cy, cy)] = jnp.where(upper, right, left)
            wide[0, m + b, pl.ds(cy, cy)] = pltpu.roll(jnp.where(upper, left, right), cy // 2, 0)


def kernel(sizes, vectors, sensors, cells_x, cells_y, window,
           records_ref, rates_in, kernel_hbm, out_ref,
           rates_ref, kbuf, recf, toep, part, got, field, packed, x_got, y_got, wide,
           d_packed, d_x_got, d_y_got, d_wide, smooth_t, pred, pred_got,
           k_sem, s_send, s_recv, h_send, h_recv, d_send, d_recv, g_send, g_recv, p_send, p_recv):
    n_s, n_x, n_y = sizes
    points = cells_x * cells_y
    chunks = min(n_s, vectors)
    per = vectors // chunks
    margin = SWEEPS
    n_q = n_x * n_y
    group = sensors // n_q
    step = 8
    steps = sensors // step
    me_s, me_x, me_y = lax.axis_index("sens"), lax.axis_index("sx"), lax.axis_index("sy")
    mine = lax.rem(me_s, chunks)
    base = me_s - mine
    me_q = me_x * n_y + me_y

    def k_copy(i):
        return pltpu.make_async_copy(
            kernel_hbm.at[pl.ds(i * step, step)], kbuf.at[pl.ds(i * step, step)], k_sem.at[i])

    for i in range(steps):
        k_copy(i).start()

    halo = Halo((n_x, n_y), cells_x, cells_y, margin)
    halo.clear(x_got, y_got)
    halo.clear(d_x_got, d_y_got)

    barrier = pltpu.get_barrier_semaphore()

    def greet_tile(k, _):
        q = lax.rem(me_q + k, n_q)
        pl.semaphore_signal(barrier, inc=1, device_id={"sx": q // n_y, "sy": lax.rem(q, n_y)}, device_id_type=MESH)
        return 0

    lax.fori_loop(1, n_q, greet_tile, 0)
    for k in range(1, n_s):
        pl.semaphore_signal(barrier, inc=1, device_id={"sens": lax.rem(me_s + k, n_s)}, device_id_type=MESH)

    anti = (lane_iota(window, window) + row_iota(window, window) == window - 1).astype(BF16)
    for v in range(vectors):
        recf[v] = jnp.dot(records_ref[v], anti, preferred_element_type=F32)

    columns = rates_in[...]
    for x in range(cells_x):
        rates_ref[0, x] = jnp.broadcast_to(columns[:, x:x + 1], (cells_y, window))
    halo.pack(rates_ref, d_packed, 1)

    pack_rows = 16
    lanes16, rows16 = lane_iota(pack_rows, window), row_iota(pack_rows, window)

    def adjoint(chunk, slot, first):
        for v in range(per):
            part[slot, v] = jnp.zeros((points, window), F32)

        def body(i, _):
            if first:
                k_copy(i).wait()
            for v in range(per):
                block = recf[chunk * per + v, pl.ds(pl.multiple_of(i * step, step), step)]
                for s in range(step):
                    line = jnp.broadcast_to(block[s:s + 1], (pack_rows, window))
                    seed = pltpu.roll(line, 0, 1, stride=1, stride_axis=0)
                    seed = jnp.where(lanes16 >= rows16, seed, 0.0)
                    for j in range(window // pack_rows):
                        shifted = seed if j == 0 else jnp.where(
                            lanes16 >= j * pack_rows, pltpu.roll(seed, j * pack_rows, 1), 0.0)
                        toep[pl.ds(s * window + j * pack_rows, pack_rows), pl.ds(v * window, window)] = shifted.astype(BF16)
            lhs = jnp.concatenate([kbuf[i * step + s] for s in range(step)], axis=1)
            res = jnp.dot(lhs, toep[...], preferred_element_type=F32)
            for v in range(per):
                part[slot, v] += res[:, v * window:(v + 1) * window]
            return 0

        lax.fori_loop(0, steps, body, 0)

    def s_copy(k, hop, v):
        return pltpu.make_async_remote_copy(
            src_ref=part.at[k, v], dst_ref=got.at[hop - 1, v],
            send_sem=s_send.at[hop - 1, v], recv_sem=s_recv.at[hop - 1, v],
            device_id={"sens": lax.rem(me_s + hop, n_s)}, device_id_type=MESH)

    halo_d = (rates_ref, d_packed, d_x_got, d_y_got, d_send, d_recv)

    def halo_f(v):
        return tuple(ref.at[v] for ref in (field, packed, x_got, y_got, h_send, h_recv))


    for k in range(1, chunks + 1):
        adjoint(lax.rem(me_s + k, chunks), k - 1, k == 1)
        if k == 1:
            pl.semaphore_wait(barrier, n_q - 1 + n_s - 1)
        for v in range(per):
            for hop in range(k, n_s, chunks):
                s_copy(k - 1, hop, v).start()
        if k == 1:
            halo.start(*halo_d)

    for v in range(per):
        for hop in range(1, n_s):
            s_copy((hop - 1) % chunks, hop, v).wait_recv()
        total = part[chunks - 1, v]
        for hop in range(1, n_s):
            total = total + got[hop - 1, v]
        field[v, 0] = total.reshape(cells_x, cells_y, window)
        halo.pack(field.at[v], packed.at[v], 1)
        halo.start(*halo_f(v))

    halo.wait(*halo_d)
    halo.assemble(rates_ref, d_x_got, d_y_got, d_wide)

    def g_copy(k, v):
        place = smooth_t.at[mine, pl.ds(v * window, window)]
        return pltpu.make_async_remote_copy(
            src_ref=place, dst_ref=place, send_sem=g_send.at[k - 1, v], recv_sem=g_recv.at[k - 1, v],
            device_id={"sens": base + lax.rem(mine + k, chunks)}, device_id_type=MESH)

    wide_rows = 2 * cells_y
    for v in range(per):
        halo.wait(*halo_f(v))
        halo.assemble(field.at[v], x_got.at[v], y_got.at[v], wide)
        now = wide[0]
        for repeat in range(SWEEPS):
            interior = now[1:-1]
            beside = now[2:] + now[:-2] + pltpu.roll(interior, wide_rows - 1, 1) + pltpu.roll(interior, 1, 1)
            rate = d_wide[0, pl.ds(repeat + 1, cells_x + 2 * (margin - repeat - 1))]
            now = interior + rate * (beside - 4.0 * interior)
        done = now[:, :cells_y].reshape(points, window).astype(BF16)
        smooth_t[mine, pl.ds(v * window, window)] = lax.dot_general(
            anti, done, (((1,), (1,)), ((), ())), preferred_element_type=F32).astype(BF16)
        for k in range(1, chunks):
            g_copy(k, v).start()

    lanes8, rows8 = lane_iota(8, window), row_iota(8, window)

    bits = n_q.bit_length() - 1

    def partner(k):
        if n_q != 1 << bits:
            return lax.rem(me_q + k, n_q)
        total = 0
        for b in range(bits):
            one, two = lax.rem(me_q // (1 << b), 2), lax.rem(k // (1 << b), 2)
            total = total + (one + two - 2 * one * two) * (1 << b)
        return total

    unroll = max(u for u in range(1, n_q + 1) if n_q % u == 0 and u * group <= 16)

    def forward(phase):
        chunk = lax.rem(mine - phase + chunks, chunks)

        def body(i, _):
            for u in range(unroll):
                q = partner(n_q - 1 - (i * unroll + u))
                rhs = jnp.concatenate([kbuf[q * group + s] for s in range(group)], axis=1)
                res = jnp.dot(smooth_t[chunk], rhs, preferred_element_type=F32)
                lines = []
                for v in range(per):
                    for s in range(group):
                        tile = res[v * window:(v + 1) * window, s * window:(s + 1) * window]
                        terms = [tile[:8]]
                        for j in range(1, window // 8):
                            cut = jnp.where(lanes8 < window - 8 * j, tile[8 * j:8 * j + 8], 0.0)
                            terms.append(pltpu.roll(cut, 8 * j, 1))
                        while len(terms) > 1:
                            terms = [a + b for a, b in zip(terms[::2], terms[1::2])]
                        run = jnp.where(lanes8 >= rows8, pltpu.roll(terms[0], 0, 1, stride=1, stride_axis=0), 0.0)
                        lines.append(jnp.sum(run, axis=0, keepdims=True))
                pred[chunk, q] = jnp.concatenate(lines, axis=0)
            for u in range(unroll):
                k = n_q - 1 - (i * unroll + u)

                @pl.when(k > 0)
                def _():
                    p_copy(phase, k).start()
            return 0

        lax.fori_loop(0, n_q // unroll, body, 0)

    def p_copy(phase, k):
        q = partner(k)
        chunk = lax.rem(mine - phase + chunks, chunks)
        return pltpu.make_async_remote_copy(
            src_ref=pred.at[chunk, q], dst_ref=pred_got.at[k - 1, chunk],
            send_sem=p_send.at[phase, k - 1], recv_sem=p_recv.at[phase, k - 1],
            device_id={"sx": q // n_y, "sy": lax.rem(q, n_y)}, device_id_type=MESH)

    for phase in range(chunks):
        for v in range(per if phase else 0):
            g_copy(phase, v).wait_recv()
        forward(phase)

    def finish(k, total):
        for phase in range(chunks):
            p_copy(phase, k).wait_recv()
        return total + pred_got[k - 1]

    out_ref[...] = lax.fori_loop(1, n_q, finish, pred[:, me_q])

    def drain(k, _):
        for phase in range(chunks):
            p_copy(phase, k).wait_send()
        return 0

    lax.fori_loop(1, n_q, drain, 0)
    for v in range(per):
        for hop in range(1, n_s):
            s_copy((hop - 1) % chunks, hop, v).wait_send()
        for k in range(1, chunks):
            g_copy(k, v).wait_send()


def per_device(sizes, records, kernel_block, diffusion):
    vectors, sensors, window = records.shape
    cells_x, cells_y = diffusion.shape
    points = cells_x * cells_y
    n_s, n_x, n_y = sizes
    n_q = n_x * n_y
    chunks = min(n_s, vectors)
    per = vectors // chunks
    group = sensors // n_q
    margin, pairs, step = SWEEPS, cells_x // 2, 8
    kernel_rows = kernel_block.reshape(sensors, points, window)
    rates = diffusion.T

    def halo_space(lead):
        return [
            pltpu.VMEM((*lead, 2, 1, pairs, cells_y, window), F32),
            pltpu.VMEM((*lead, 2, 1, margin, cells_y, window), F32),
            pltpu.VMEM((*lead, 2, 1, pairs + margin, cells_y, window), F32),
            pltpu.VMEM((1, cells_x + 2 * margin, 2 * cells_y, window), F32),
        ]

    dma = pltpu.SemaphoreType.DMA
    out = pl.pallas_call(
        functools.partial(kernel, sizes, vectors, sensors, cells_x, cells_y, window),
        out_shape=jax.ShapeDtypeStruct((chunks, per * group, window), F32),
        in_specs=[
            pl.BlockSpec(memory_space=pltpu.VMEM),
            pl.BlockSpec(memory_space=pltpu.VMEM),
            pl.BlockSpec(memory_space=pl.ANY),
        ],
        out_specs=pl.BlockSpec(memory_space=pltpu.VMEM),
        scratch_shapes=[
            pltpu.VMEM((1, cells_x, cells_y, window), F32),
            pltpu.VMEM((sensors, points, window), BF16),
            pltpu.VMEM((vectors, sensors, window), F32),
            pltpu.VMEM((step * window, per * window), BF16),
            pltpu.VMEM((chunks, per, points, window), F32),
            pltpu.VMEM((max(n_s - 1, 1), per, points, window), F32),
            pltpu.VMEM((per, 1, cells_x, cells_y, window), F32),
            *halo_space((per,)),
            *halo_space(()),
            pltpu.VMEM((chunks, per * window, points), BF16),
            pltpu.VMEM((chunks, n_q, per * group, window), F32),
            pltpu.VMEM((max(n_q - 1, 1), chunks, per * group, window), F32),
            dma((sensors // step,)),
            *[dma((max(n_s - 1, 1), per))] * 2,
            *[dma((per, len(DIRECTIONS)))] * 2,
            *[dma((len(DIRECTIONS),))] * 2,
            *[dma((max(chunks - 1, 1), per))] * 2,
            *[dma((chunks, max(n_q - 1, 1)))] * 2,
        ],
        compiler_params=pltpu.CompilerParams(collective_id=0, has_side_effects=True),
    )(records, rates, kernel_rows)
    return out.reshape(vectors, group, window)


def solution(mesh):
    sizes = tuple(mesh.shape[a] for a in ("sens", "sx", "sy"))
    return jax.shard_map(
        functools.partial(per_device, sizes),
        mesh=mesh,
        in_specs=(P(None, "sens", None), P("sens", "sx", "sy", None), P("sx", "sy")),
        out_specs=P(None, ("sens", "sx", "sy"), None),
        check_vma=False,
    )
```
